32 devices in a mesh: group: 2 (over y), tm: 4 (over x, core), space: 4 (over z).
Axes of the slice: x: 2, y: 2, z: 4, core: 2. Of those that a mesh axis runs over, the one named last changes fastest.
Arguments:
- latent: bfloat16 [8, 16, 4, 128], P(('group', 'tm'), None, 'space'), parts along dimension 0, may hold values from -27 to 27
- conv_weight: bfloat16 [3, 3, 3, 16, 512], replicated, may hold values from -0.3125 to 0.3125
- norm_gain: float32 [512], replicated, may hold values from 0.25 to 1.75
- qkv_weight: bfloat16 [512, 1536], replicated, may hold values from -0.25 to 0.25
- out_weight: bfloat16 [512, 512], replicated, may hold values from -0.25 to 0.25
- grad_out: bfloat16 [8, 4, 128, 512], P(('group', 'tm'), 'space'), parts along dimension 0, may hold values from -6 to 6
Outputs:
- grad_latent: float32 [8, 16, 4, 128], P(('group', 'tm'), None, 'space'), parts along dimension 0
The draws below stay inside these ranges and needn't reach their ends.
There are 2 independent parts, one for each index of `group`. The reference program is written for one: setup_inputs(seed, part) draws one part's arguments, and reference() takes and returns one part's arrays. A program takes and returns all parts, laid end to end along the dimension named above; an argument that names none is the same for every part. Nothing has to cross between parts.
All inputs are finite; a program needn't handle non-finite values.
Results may differ from the reference program's by a relative error of at most 0.013.
The reference program's roundings to bfloat16 on the way count: a program that leaves them out, or rounds other values in their place, can miss the bound.
Values may be sent and summed in bfloat16 or wider, within the bound.
A program may use at most 64 MiB of HBM per device.

```python
import jax
import jax.numpy as jnp
from jax import lax

C = 512
LAT = 16
GROUPS = 32
WIDTH = 128
FRAMES = 4
HEIGHT = 4


def draw_latent(key, part):
    shape = (FRAMES, LAT, HEIGHT, WIDTH)
    base_key, chan_key = jax.random.split(key, 2)
    heights = jnp.arange(HEIGHT, dtype=jnp.float32) / max(HEIGHT - 1, 1)
    channel_scale = jnp.exp(jax.random.uniform(chan_key, (FRAMES, LAT, 1, 1), jnp.float32, -0.7, 0.7))
    values_raw = jax.random.truncated_normal(base_key, -4.0, 4.0, shape, jnp.float32)
    row_scale = 3.0 ** heights
    values_raw = values_raw * 0.0625
    return (values_raw * channel_scale * row_scale[None, None, :, None]).astype(jnp.bfloat16)


def draw_grad_out(key, part):
    shape = (FRAMES, HEIGHT, WIDTH, C)
    base_key, shift_key = jax.random.split(key)
    offset = jnp.clip(0.5 * jax.random.normal(shift_key, (FRAMES, 1, 1, C), jnp.float32), -2.0, 2.0)
    base_values = jax.random.truncated_normal(base_key, -4.0, 4.0, shape, jnp.float32)
    return (base_values + offset).astype(jnp.bfloat16)


def centred(own_key, extent, width, bound, kind=jnp.bfloat16):
    values = width * jax.random.normal(own_key, extent, jnp.float32)
    return jnp.clip(values, min=-bound, max=bound).astype(kind)


def setup_inputs(seed: int = 0, part: int = 0) -> dict:
    key_list = jax.random.split(jax.random.key(seed), 7)
    own_keys = jax.random.split(jax.random.fold_in(key_list[6], part), 7)
    return {
        "latent": draw_latent(jax.random.fold_in(jax.random.fold_in(key_list[6], part), 71), part),
        "conv_weight": centred(key_list[1], (3, 3, 3, LAT, C), (27 * LAT) ** -0.5, 0.3125),
        "norm_gain": jnp.clip(1.0 + 0.15 * jax.random.normal(key_list[2], (C,), jnp.float32), 0.25, 1.75),
        "qkv_weight": centred(key_list[3], (C, 3 * C), C ** -0.5, 0.25),
        "out_weight": centred(key_list[4], (C, C), C ** -0.5, 0.25),
        "grad_out": draw_grad_out(jax.random.fold_in(jax.random.fold_in(key_list[6], part), 71), part),
    }


EPSILON = 1e-06

def frame_attention(frame_items):
    query_rows, key_rows, value_rows, grad_att = frame_items
    scaling = C ** (-0.5)
    scores = jnp.dot(query_rows, key_rows.T, preferred_element_type=jnp.float32) * scaling
    largest = lax.optimization_barrier(jnp.max(scores, axis=1))
    log_norm = largest + jnp.log(lax.optimization_barrier(jnp.sum(jnp.exp(scores - largest[:, None]), axis=1)))
    soft_probs = jnp.exp(scores - log_norm[:, None])
    soft_bf = soft_probs.astype(jnp.bfloat16)
    attended = jnp.dot(soft_bf, value_rows, preferred_element_type=jnp.float32).astype(jnp.bfloat16)
    attended = lax.optimization_barrier(attended)
    row_delta = lax.optimization_barrier(jnp.sum(grad_att.astype(jnp.float32) * attended.astype(jnp.float32), axis=1))
    grad_probs = jnp.dot(grad_att, value_rows.T, preferred_element_type=jnp.float32)
    dscore = (soft_probs * (grad_probs - row_delta[:, None]) * scaling).astype(jnp.bfloat16)
    grad_query = jnp.dot(dscore, key_rows, preferred_element_type=jnp.float32).astype(jnp.bfloat16)
    grad_keys = jnp.dot(dscore.T, query_rows, preferred_element_type=jnp.float32).astype(jnp.bfloat16)
    grad_values = jnp.dot(soft_bf.T, grad_att, preferred_element_type=jnp.float32).astype(jnp.bfloat16)
    return jnp.concatenate([grad_query, grad_keys, grad_values], axis=1)

def reference(latent, conv_weight, norm_gain, qkv_weight, out_weight, grad_out):
    conv_flat = conv_weight.reshape(27 * LAT, C)
    channels_last = jnp.transpose(latent, (0, 2, 3, 1))
    padded = jnp.pad(channels_last, ((2, 0), (1, 1), (1, 1), (0, 0)))
    pieces = [padded[2 - a:2 - a + FRAMES, b:b + HEIGHT, e:e + WIDTH, :] for a in range(3) for b in range(3) for e in range(3)]
    patches = jnp.concatenate(pieces, axis=-1).reshape(-1, 27 * LAT)
    hidden = jnp.dot(patches, conv_flat, preferred_element_type=jnp.float32)
    frame_cells = HEIGHT * WIDTH
    per_group = C // GROUPS
    grouped = hidden.reshape(FRAMES, frame_cells, GROUPS, per_group)
    average = lax.optimization_barrier(jnp.mean(grouped, axis=(1, 3), keepdims=True))
    spread = lax.optimization_barrier(jnp.mean(jnp.square(grouped - average), axis=(1, 3), keepdims=True))
    inverse = lax.rsqrt(spread + EPSILON)
    unit_cells = (grouped - average) * inverse
    gain_grid = norm_gain.reshape(GROUPS, per_group)
    normed = (unit_cells * gain_grid).astype(jnp.bfloat16).reshape(-1, C)
    projected = jnp.dot(normed, qkv_weight, preferred_element_type=jnp.float32).astype(jnp.bfloat16)
    projected = projected.reshape(FRAMES, frame_cells, 3 * C)
    upstream = grad_out.reshape(-1, C)
    grad_att = jnp.dot(upstream, out_weight.T, preferred_element_type=jnp.float32).astype(jnp.bfloat16)
    grad_att = grad_att.reshape(FRAMES, frame_cells, C)
    grad_proj = lax.map(frame_attention, (projected[:, :, :C], projected[:, :, C:2 * C], projected[:, :, 2 * C:], grad_att))
    grad_normed = jnp.dot(grad_proj.reshape(-1, 3 * C), qkv_weight.T, preferred_element_type=jnp.float32)
    scaled = grad_normed.reshape(FRAMES, frame_cells, GROUPS, per_group) * gain_grid
    first_mean = lax.optimization_barrier(jnp.mean(scaled, axis=(1, 3), keepdims=True))
    second_mean = lax.optimization_barrier(jnp.mean(scaled * unit_cells, axis=(1, 3), keepdims=True))
    grad_hidden = upstream.astype(jnp.float32).reshape(FRAMES, frame_cells, GROUPS, per_group)
    grad_hidden = grad_hidden + (scaled - first_mean - unit_cells * second_mean) * inverse
    grad_hidden = grad_hidden.astype(jnp.bfloat16).reshape(-1, C)
    columns = jnp.dot(grad_hidden, conv_flat.T, preferred_element_type=jnp.float32)
    columns = columns.reshape(FRAMES, HEIGHT, WIDTH, 27, LAT)
    columns = jnp.pad(columns, ((0, 2), (1, 1), (1, 1), (0, 0), (0, 0)))
    summed = jnp.zeros((FRAMES, HEIGHT, WIDTH, LAT), jnp.float32)
    tap_index = 0
    for a in range(3):
        for b in range(3):
            for e in range(3):
                summed = summed + columns[a:a + FRAMES, 2 - b:2 - b + HEIGHT, 2 - e:2 - e + WIDTH, tap_index]
                tap_index = tap_index + 1
    return jnp.transpose(summed, (0, 3, 1, 2))
```

```python
import functools

import jax
import jax.numpy as jnp
from jax import lax
from jax.experimental import pallas as pl
from jax.experimental.pallas import tpu as pltpu
from jax.sharding import PartitionSpec as P

GROUPS = 32
EPSILON = 1e-06
BACK = 3
LANES = 128
MESH = pl.DeviceIdType.MESH


def dot(left, right, left_dim, right_dim):
    return lax.dot_general(
        left, right, (((left_dim,), (right_dim,)), ((), ())), preferred_element_type=jnp.float32
    )


def group_sums(rows, per_group):
    channels = rows[0].shape[1]
    tiles = channels // LANES
    packed = jnp.concatenate(
        [row[:, k * LANES : (k + 1) * LANES] for row in rows for k in range(tiles)], axis=0
    )
    lane = lax.broadcasted_iota(jnp.int32, packed.shape, 1)
    step = 1
    while step < per_group:
        upper = pltpu.roll(packed, step, 1)
        lower = pltpu.roll(packed, LANES - step, 1)
        packed = packed + jnp.where((lane & step) != 0, upper, lower)
        step *= 2
    return [
        jnp.concatenate([packed[i * tiles + k : i * tiles + k + 1] for k in range(tiles)], axis=1)
        for i in range(len(rows))
    ]


def shifted(value, by):
    if by == 0:
        return value
    lane = lax.broadcasted_iota(jnp.int32, value.shape, 1)
    keep = lane < LANES - 1 if by == 1 else lane > 0
    return jnp.where(keep, pltpu.roll(value, (-by) % LANES, 1), 0.0)


def chunked(count, body, carry):
    if count == 1:
        return body(0, carry)
    return lax.fori_loop(0, count, body, carry)


def kernel(
    frames, rows, chunk,
    lat_hbm, conv_hbm, gain_hbm, qkv_hbm, out_hbm, grad_hbm,
    result_ref,
    lat, conv, gain, qkv, outw, grad,
    window, patches, unit, normed, keyval, scores, products, soft, dscore, grad_kv, grad_norm,
    grad_hid, columns, partial, arrived,
    load_sem, lat_send, lat_recv, part_send, part_recv,
):
    t = lax.axis_index("tm")
    me = lax.axis_index("space")
    lat_width = lat.shape[0]
    channels = grad.shape[1]
    per_group = channels // GROUPS
    cells = rows * LANES
    chunks = cells // chunk
    scaling = channels ** (-0.5)
    own = pl.ds(pl.multiple_of(me * LANES, LANES), LANES)

    loads = [
        pltpu.make_async_copy(source, target, load_sem.at[i])
        for i, (source, target) in enumerate(
            [(lat_hbm, lat), (grad_hbm, grad), (out_hbm, outw), (conv_hbm, conv), (gain_hbm, gain), (qkv_hbm, qkv)]
        )
    ]
    for load in loads:
        load.start()

    barrier = pltpu.get_barrier_semaphore()
    for step in range(1 - BACK, BACK):
        for d in range(rows):
            if step == 0 and d == 0:
                continue

            @pl.when((t + step >= 0) & (t + step < frames))
            def _(step=step, d=d):
                pl.semaphore_signal(
                    barrier, inc=1,
                    device_id={"tm": t + step, "space": lax.rem(me + d, rows)},
                    device_id_type=MESH,
                )

    loads[0].wait()
    window[0, me] = lat[...]
    for a in range(1, BACK):

        @pl.when(t < a)
        def _(a=a):
            window[a] = jnp.zeros(window.shape[1:], window.dtype)

    near = jnp.minimum(t, BACK - 1) + jnp.minimum(frames - 1 - t, BACK - 1) + 1
    pl.semaphore_wait(barrier, near * rows - 1)

    def latent_copy(a, row, slot):
        return pltpu.make_async_remote_copy(
            src_ref=lat,
            dst_ref=window.at[a, slot],
            send_sem=lat_send.at[a, row],
            recv_sem=lat_recv.at[a, slot],
            device_id={"tm": t + a, "space": row},
            device_id_type=MESH,
        )

    pairs = [(a, d) for a in range(BACK) for d in range(rows) if a or d]
    for a, d in pairs:

        @pl.when(t + a < frames)
        def _(a=a, d=d):
            latent_copy(a, lax.rem(me + d, rows), me).start()

    loads[1].wait()
    loads[2].wait()
    grad_att = dot(grad[...], outw[...], 1, 1).astype(jnp.bfloat16)

    for a, d in pairs:

        @pl.when(t >= a)
        def _(a=a, d=d):
            slot = lax.rem(me + d, rows)
            latent_copy(a, slot, slot).wait_recv()

    zero_slab = jnp.zeros((3 * lat_width, LANES), jnp.bfloat16)
    for a in range(BACK):
        for r in range(rows):
            piece = window[a, r].astype(jnp.float32)
            for e in range(3):
                moved = shifted(piece, e - 1).astype(jnp.bfloat16)
                for b in range(3):
                    target = r - b + 1
                    if 0 <= target < rows:
                        tap = (a * 9 + b * 3 + e) * lat_width
                        patches[tap : tap + lat_width, target * LANES : (target + 1) * LANES] = moved
        first = a * 9 * lat_width
        patches[first : first + 3 * lat_width, 0:LANES] = zero_slab
        last = (a * 9 + 6) * lat_width
        patches[last : last + 3 * lat_width, (rows - 1) * LANES : rows * LANES] = zero_slab

    loads[3].wait()
    loads[4].wait()

    def rows_of(i):
        if isinstance(i, int):
            return pl.ds(i * chunk, chunk)
        return pl.ds(pl.multiple_of(i * chunk, chunk), chunk)

    zero_row = jnp.zeros((1, channels), jnp.float32)

    def convolve(i, total):
        part = dot(patches[:, rows_of(i)], conv[...], 0, 0)
        unit[rows_of(i), :] = part
        return total + jnp.sum(part, axis=0, keepdims=True)

    count = float(cells * per_group)
    (average,) = group_sums([chunked(chunks, convolve, zero_row)], per_group)
    average = average / count

    def square(i, total):
        away = unit[rows_of(i), :] - average
        return total + jnp.sum(away * away, axis=0, keepdims=True)

    (spread,) = group_sums([chunked(chunks, square, zero_row)], per_group)
    inverse = lax.rsqrt(spread / count + EPSILON)
    gains = gain[...]

    def normalise(i, carry):
        value = (unit[rows_of(i), :] - average) * inverse
        unit[rows_of(i), :] = value
        normed[rows_of(i), :] = (value * gains).astype(jnp.bfloat16)
        return carry

    chunked(chunks, normalise, 0)

    loads[5].wait()
    query = dot(normed[own, :], qkv[:, :channels], 1, 0).astype(jnp.bfloat16)

    def project(i, highest):
        keyval[rows_of(i), :] = dot(normed[rows_of(i), :], qkv[:, channels:], 1, 0).astype(jnp.bfloat16)
        part = dot(keyval[rows_of(i), :channels], query, 1, 1) * scaling
        scores[rows_of(i), :] = part
        products[rows_of(i), :] = dot(keyval[rows_of(i), channels:], grad_att, 1, 1)
        return jnp.maximum(highest, jnp.max(part, axis=0, keepdims=True))

    highest = chunked(chunks, project, jnp.full((1, LANES), -jnp.inf, jnp.float32))

    def exponent(i, total):
        part = jnp.exp(scores[rows_of(i), :] - highest)
        scores[rows_of(i), :] = part
        return total + jnp.sum(part, axis=0, keepdims=True)

    share = 1.0 / chunked(chunks, exponent, jnp.zeros((1, LANES), jnp.float32))

    def normal(i, total):
        part = scores[rows_of(i), :] * share
        scores[rows_of(i), :] = part
        rounded = part.astype(jnp.bfloat16)
        soft[rows_of(i), :] = rounded
        return total + jnp.sum(rounded.astype(jnp.float32) * products[rows_of(i), :], axis=0, keepdims=True)

    delta = chunked(chunks, normal, jnp.zeros((1, LANES), jnp.float32))

    def backward(i, total):
        part = scores[rows_of(i), :] * (products[rows_of(i), :] - delta) * scaling
        rounded = part.astype(jnp.bfloat16)
        dscore[rows_of(i), :] = rounded
        grad_kv[rows_of(i), :channels] = dot(rounded, query, 1, 0).astype(jnp.bfloat16)
        grad_kv[rows_of(i), channels:] = dot(soft[rows_of(i), :], grad_att, 1, 0).astype(jnp.bfloat16)
        grad_norm[rows_of(i), :] = dot(grad_kv[rows_of(i), :], qkv[:, channels:], 1, 1)
        return total + dot(rounded, keyval[rows_of(i), :channels], 0, 0)

    grad_query = chunked(chunks, backward, jnp.zeros((LANES, channels), jnp.float32))
    grad_norm[own, :] += dot(grad_query.astype(jnp.bfloat16), qkv[:, :channels], 1, 1)

    def moments(i, carry):
        first, second = carry
        part = grad_norm[rows_of(i), :]
        first = first + jnp.sum(part, axis=0, keepdims=True)
        second = second + jnp.sum(part * unit[rows_of(i), :], axis=0, keepdims=True)
        return first, second

    first, second = chunked(chunks, moments, (zero_row, zero_row))
    first, second = group_sums([first * gains, second * gains], per_group)
    first = first / count
    second = second / count

    def hidden_grad(where):
        return (grad_norm[where, :] * gains - first - unit[where, :] * second) * inverse

    def finish(i, carry):
        grad_hid[rows_of(i), :] = hidden_grad(rows_of(i)).astype(jnp.bfloat16)
        return carry

    chunked(chunks, finish, 0)
    grad_hid[own, :] = (grad[...].astype(jnp.float32) + hidden_grad(own)).astype(jnp.bfloat16)

    columns[:, 0:LANES] = jnp.zeros((columns.shape[0], LANES), jnp.float32)
    columns[:, (rows + 1) * LANES :] = jnp.zeros((columns.shape[0], LANES), jnp.float32)

    def spread_taps(i, carry):
        if isinstance(i, int):
            where = pl.ds(LANES + i * chunk, chunk)
        else:
            where = pl.ds(pl.multiple_of(LANES + i * chunk, LANES), chunk)
        columns[:, where] = dot(conv[...], grad_hid[rows_of(i), :], 1, 1)
        return carry

    chunked(chunks, spread_taps, 0)

    def partial_copy(a, row, slot):
        return pltpu.make_async_remote_copy(
            src_ref=partial.at[a, row],
            dst_ref=arrived.at[a, slot],
            send_sem=part_send.at[a, row],
            recv_sem=part_recv.at[a, slot],
            device_id={"tm": t - a, "space": row},
            device_id_type=MESH,
        )

    for a in reversed(range(BACK)):
        for y in range(rows):
            total = jnp.zeros((lat_width, LANES), jnp.float32)
            for e in range(3):
                inner = jnp.zeros((lat_width, LANES), jnp.float32)
                for b in range(3):
                    tap = (a * 9 + b * 3 + e) * lat_width
                    at = (y - b + 2) * LANES
                    inner = inner + columns[tap : tap + lat_width, at : at + LANES]
                total = total + shifted(inner, 1 - e)
            partial[a, y] = total
        for d in range(rows):
            if a or d:

                @pl.when(t >= a)
                def _(a=a, d=d):
                    partial_copy(a, lax.rem(me + d, rows), me).start()

    arrived[0, me] = partial[0, me]
    for a in range(1, BACK):

        @pl.when(t + a >= frames)
        def _(a=a):
            arrived[a] = jnp.zeros(arrived.shape[1:], arrived.dtype)

    for a, d in pairs:

        @pl.when(t + a < frames)
        def _(a=a, d=d):
            slot = lax.rem(me + d, rows)
            partial_copy(a, slot, slot).wait_recv()

    total = jnp.zeros((lat_width, LANES), jnp.float32)
    for a in range(BACK):
        for r in range(rows):
            total = total + arrived[a, r]
    result_ref[...] = total

    for a, d in pairs:

        @pl.when(t + a < frames)
        def _(a=a, d=d):
            latent_copy(a, lax.rem(me + d, rows), me).wait_send()

        @pl.when(t >= a)
        def _(a=a, d=d):
            partial_copy(a, lax.rem(me + d, rows), me).wait_send()


def on_device(frames, rows, latent, conv_weight, norm_gain, qkv_weight, out_weight, grad_out):
    lat_width = latent.shape[1]
    channels = grad_out.shape[3]
    taps = 27 * lat_width
    cells = rows * LANES
    chunk = min(cells, 512)
    bf16, f32 = jnp.bfloat16, jnp.float32
    flat = (
        latent.reshape(lat_width, LANES),
        conv_weight.reshape(taps, channels),
        norm_gain.reshape(1, channels),
        qkv_weight,
        out_weight,
        grad_out.reshape(LANES, channels),
    )
    scratch = [pltpu.VMEM(value.shape, value.dtype) for value in flat]
    scratch += [
        pltpu.VMEM((BACK, rows, lat_width, LANES), bf16),
        pltpu.VMEM((taps, cells), bf16),
        pltpu.VMEM((cells, channels), f32),
        pltpu.VMEM((cells, channels), bf16),
        pltpu.VMEM((cells, 2 * channels), bf16),
        pltpu.VMEM((cells, LANES), f32),
        pltpu.VMEM((cells, LANES), f32),
        pltpu.VMEM((cells, LANES), bf16),
        pltpu.VMEM((cells, LANES), bf16),
        pltpu.VMEM((cells, 2 * channels), bf16),
        pltpu.VMEM((cells, channels), f32),
        pltpu.VMEM((cells, channels), bf16),
        pltpu.VMEM((taps, cells + 2 * LANES), f32),
        pltpu.VMEM((BACK, rows, lat_width, LANES), f32),
        pltpu.VMEM((BACK, rows, lat_width, LANES), f32),
        pltpu.SemaphoreType.DMA((6,)),
        pltpu.SemaphoreType.DMA((BACK, rows)),
        pltpu.SemaphoreType.DMA((BACK, rows)),
        pltpu.SemaphoreType.DMA((BACK, rows)),
        pltpu.SemaphoreType.DMA((BACK, rows)),
    ]
    result = pl.pallas_call(
        functools.partial(kernel, frames, rows, chunk),
        out_shape=jax.ShapeDtypeStruct((lat_width, LANES), f32),
        in_specs=[pl.BlockSpec(memory_space=pl.ANY)] * 6,
        out_specs=pl.BlockSpec(memory_space=pltpu.VMEM),
        scratch_shapes=scratch,
        compiler_params=pltpu.CompilerParams(
            collective_id=0, has_side_effects=True, vmem_limit_bytes=56 * 2**20
        ),
    )(*flat)
    return result.reshape(1, lat_width, 1, LANES)


def solution(mesh):
    return jax.shard_map(
        functools.partial(on_device, mesh.shape["tm"], mesh.shape["space"]),
        mesh=mesh,
        in_specs=(
            P(("group", "tm"), None, "space", None),
            P(),
            P(),
            P(),
            P(),
            P(("group", "tm"), "space", None, None),
        ),
        out_specs=P(("group", "tm"), None, "space", None),
        check_vma=False,
    )
```

```python
import functools

import jax
import jax.numpy as jnp
from jax import lax
from jax.experimental import pallas as pl
from jax.experimental.pallas import tpu as pltpu
from jax.sharding import PartitionSpec as P

GROUPS = 32
EPSILON = 1e-06
BACK = 3
LANES = 128
MESH = pl.DeviceIdType.MESH


def dot(left, right, left_dim, right_dim):
    return lax.dot_general(
        left, right, (((left_dim,), (right_dim,)), ((), ())), preferred_element_type=jnp.float32
    )


def group_sums(rows, per_group):
    channels = rows[0].shape[1]
    tiles = channels // LANES
    packed = jnp.concatenate(
        [row[:, k * LANES : (k + 1) * LANES] for row in rows for k in range(tiles)], axis=0
    )
    lane = lax.broadcasted_iota(jnp.int32, packed.shape, 1)
    step = 1
    while step < per_group:
        upper = pltpu.roll(packed, step, 1)
        lower = pltpu.roll(packed, LANES - step, 1)
        packed = packed + jnp.where((lane & step) != 0, upper, lower)
        step *= 2
    return [
        jnp.concatenate([packed[i * tiles + k : i * tiles + k + 1] for k in range(tiles)], axis=1)
        for i in range(len(rows))
    ]


def shifted(value, by):
    if by == 0:
        return value
    lane = lax.broadcasted_iota(jnp.int32, value.shape, 1)
    keep = lane < LANES - 1 if by == 1 else lane > 0
    return jnp.where(keep, pltpu.roll(value, (-by) % LANES, 1), 0.0)


def chunked(count, body, carry):
    if count == 1:
        return body(0, carry)
    return lax.fori_loop(0, count, body, carry)


def kernel(
    frames, rows, chunk,
    lat_hbm, conv_hbm, gain_hbm, qkv_hbm, out_hbm, grad_hbm,
    result_ref,
    lat, conv, gain, qkv, outw, grad,
    window, patches, unit, normed, mixed, pair, scored, weights, grad_norm,
    grad_hid, columns, partial, arrived,
    load_sem, lat_send, lat_recv, part_send, part_recv,
):
    t = lax.axis_index("tm")
    me = lax.axis_index("space")
    lat_width = lat.shape[0]
    channels = grad.shape[1]
    per_group = channels // GROUPS
    cells = rows * LANES
    chunks = cells // chunk
    scaling = channels ** (-0.5)
    own = pl.ds(pl.multiple_of(me * LANES, LANES), LANES)

    loads = [
        pltpu.make_async_copy(source, target, load_sem.at[i])
        for i, (source, target) in enumerate(
            [(lat_hbm, lat), (grad_hbm, grad), (out_hbm, outw), (qkv_hbm, qkv), (conv_hbm, conv), (gain_hbm, gain)]
        )
    ]
    loads[0].start()

    def other(k):
        if k == rows - 1:
            return me
        upper = rows - 1 - k
        return jnp.where(2 * me >= rows, jnp.where(k >= me, k + 1, k), jnp.where(upper <= me, upper - 1, upper))

    barrier = pltpu.get_barrier_semaphore()
    def greet(step):
        for k in range(rows if step else rows - 1):
            pl.semaphore_signal(
                barrier, inc=1, device_id={"tm": t + step, "space": other(k)}, device_id_type=MESH
            )

    greet(0)
    for step in range(1, BACK):
        pl.when(t + step < frames)(functools.partial(greet, step))
        pl.when(t >= step)(functools.partial(greet, -step))
    for load in loads[1:]:
        load.start()

    loads[0].wait()
    window[0, me] = lat[...]
    for a in range(1, BACK):

        @pl.when(t < a)
        def _(a=a):
            window[a] = jnp.zeros(window.shape[1:], window.dtype)

    near = jnp.minimum(t, BACK - 1) + jnp.minimum(frames - 1 - t, BACK - 1) + 1
    pl.semaphore_wait(barrier, near * rows - 1)

    def send(source, target, send_sem, recv_sem, frame, row):
        return pltpu.make_async_remote_copy(
            src_ref=source, dst_ref=target, send_sem=send_sem, recv_sem=recv_sem,
            device_id={"tm": frame, "space": row}, device_id_type=MESH,
        )

    def whole(buffer, a, send_sem, recv_sem):
        block = buffer.at[a] if a else buffer.at[a, 0 : rows - 1]
        return send(block, block, send_sem.at[a], recv_sem.at[a], t, me)

    def send_latent(a):
        for k in range(rows if a else rows - 1):
            send(lat, window.at[a, me], lat_send.at[a], lat_recv.at[a], t + a, other(k)).start()

    for a in reversed(range(BACK)):
        pl.when(t + a < frames)(functools.partial(send_latent, a))

    loads[1].wait()
    loads[2].wait()
    grad_att = dot(grad[...], outw[...], 1, 1).astype(jnp.bfloat16)
    loads[3].wait()
    pair[LANES:, :] = dot(grad_att, qkv[:, 2 * channels :], 1, 1).astype(jnp.bfloat16)
    mixed[...] = dot(qkv[:, :channels], qkv[:, channels : 2 * channels], 1, 1).astype(jnp.bfloat16)
    loads[4].wait()
    loads[5].wait()

    for a in range(BACK):
        pl.when(t >= a)(lambda a=a: whole(window, a, lat_send, lat_recv).wait_recv())

    zero_slab = jnp.zeros((3 * lat_width, LANES), jnp.bfloat16)
    for a in range(BACK):
        for r in range(rows):
            piece = window[a, r].astype(jnp.float32)
            for e in range(3):
                moved = shifted(piece, e - 1).astype(jnp.bfloat16)
                for b in range(3):
                    target = r - b + 1
                    if 0 <= target < rows:
                        tap = (a * 9 + b * 3 + e) * lat_width
                        patches[tap : tap + lat_width, target * LANES : (target + 1) * LANES] = moved
        first = a * 9 * lat_width
        patches[first : first + 3 * lat_width, 0:LANES] = zero_slab
        last = (a * 9 + 6) * lat_width
        patches[last : last + 3 * lat_width, (rows - 1) * LANES : rows * LANES] = zero_slab

    def rows_of(i):
        if isinstance(i, int):
            return pl.ds(i * chunk, chunk)
        return pl.ds(pl.multiple_of(i * chunk, chunk), chunk)

    zero_row = jnp.zeros((1, channels), jnp.float32)

    def convolve(i, total):
        part = dot(patches[:, rows_of(i)], conv[...], 0, 0)
        unit[rows_of(i), :] = part
        return total + jnp.sum(part, axis=0, keepdims=True)

    count = float(cells * per_group)
    (average,) = group_sums([chunked(chunks, convolve, zero_row)], per_group)
    average = average / count

    def square(i, total):
        away = unit[rows_of(i), :] - average
        return total + jnp.sum(away * away, axis=0, keepdims=True)

    (spread,) = group_sums([chunked(chunks, square, zero_row)], per_group)
    inverse = lax.rsqrt(spread / count + EPSILON)
    gains = gain[...]

    def normalise(i, carry):
        value = (unit[rows_of(i), :] - average) * inverse
        unit[rows_of(i), :] = value
        normed[rows_of(i), :] = (value * gains).astype(jnp.bfloat16)
        return carry

    chunked(chunks, normalise, 0)

    pair[:LANES, :] = dot(normed[own, :], mixed[...], 1, 0).astype(jnp.bfloat16)

    def score(i, highest):
        part = dot(normed[rows_of(i), :], pair[...], 1, 1)
        scored[rows_of(i), :] = part
        return jnp.maximum(highest, jnp.max(part[:, :LANES], axis=0, keepdims=True))

    highest = chunked(chunks, score, jnp.full((1, LANES), -jnp.inf, jnp.float32))

    def exponent(i, total):
        part = jnp.exp((scored[rows_of(i), :LANES] - highest) * scaling)
        scored[rows_of(i), :LANES] = part
        return total + jnp.sum(part, axis=0, keepdims=True)

    share = 1.0 / chunked(chunks, exponent, jnp.zeros((1, LANES), jnp.float32))

    def normal(i, total):
        part = scored[rows_of(i), :LANES] * share
        scored[rows_of(i), :LANES] = part
        rounded = part.astype(jnp.bfloat16)
        weights[rows_of(i), LANES:] = rounded
        return total + jnp.sum(rounded.astype(jnp.float32) * scored[rows_of(i), LANES:], axis=0, keepdims=True)

    delta = chunked(chunks, normal, jnp.zeros((1, LANES), jnp.float32))

    def backward(i, total):
        part = scored[rows_of(i), :LANES] * (scored[rows_of(i), LANES:] - delta) * scaling
        rounded = part.astype(jnp.bfloat16)
        weights[rows_of(i), :LANES] = rounded
        grad_norm[rows_of(i), :] = dot(weights[rows_of(i), :], pair[...], 1, 0)
        return total + dot(rounded, normed[rows_of(i), :], 0, 0)

    pulled = chunked(chunks, backward, jnp.zeros((LANES, channels), jnp.float32))
    grad_norm[own, :] += dot(pulled.astype(jnp.bfloat16), mixed[...], 1, 1)

    def moments(i, carry):
        first, second = carry
        part = grad_norm[rows_of(i), :]
        first = first + jnp.sum(part, axis=0, keepdims=True)
        second = second + jnp.sum(part * unit[rows_of(i), :], axis=0, keepdims=True)
        return first, second

    first, second = chunked(chunks, moments, (zero_row, zero_row))
    first, second = group_sums([first * gains, second * gains], per_group)
    first = first / count
    second = second / count

    def hidden_grad(where):
        return (grad_norm[where, :] * gains - first - unit[where, :] * second) * inverse

    def finish(i, carry):
        grad_hid[rows_of(i), :] = hidden_grad(rows_of(i)).astype(jnp.bfloat16)
        return carry

    chunked(chunks, finish, 0)
    grad_hid[own, :] = (grad[...].astype(jnp.float32) + hidden_grad(own)).astype(jnp.bfloat16)

    columns[:, 0:LANES] = jnp.zeros((columns.shape[0], LANES), jnp.float32)
    columns[:, (rows + 1) * LANES :] = jnp.zeros((columns.shape[0], LANES), jnp.float32)

    def spread_taps(i, carry):
        if isinstance(i, int):
            where = pl.ds(LANES + i * chunk, chunk)
        else:
            where = pl.ds(pl.multiple_of(LANES + i * chunk, LANES), chunk)
        columns[:, where] = dot(conv[...], grad_hid[rows_of(i), :], 1, 1)
        return carry

    chunked(chunks, spread_taps, 0)

    def send_partial(a):
        for k in range(rows if a else rows - 1):
            row = other(k)
            send(partial.at[a, row], arrived.at[a, me], part_send.at[a], part_recv.at[a], t - a, row).start()

    for a in reversed(range(BACK)):
        for y in range(rows):
            total = jnp.zeros((lat_width, LANES), jnp.float32)
            for e in range(3):
                inner = jnp.zeros((lat_width, LANES), jnp.float32)
                for b in range(3):
                    tap = (a * 9 + b * 3 + e) * lat_width
                    at = (y - b + 2) * LANES
                    inner = inner + columns[tap : tap + lat_width, at : at + LANES]
                total = total + shifted(inner, 1 - e)
            partial[a, y] = total
        pl.when(t >= a)(functools.partial(send_partial, a))

    arrived[0, me] = partial[0, me]
    for a in range(1, BACK):

        @pl.when(t + a >= frames)
        def _(a=a):
            arrived[a] = jnp.zeros(arrived.shape[1:], arrived.dtype)

    for a in range(BACK):
        pl.when(t + a < frames)(lambda a=a: whole(arrived, a, part_send, part_recv).wait_recv())

    total = jnp.zeros((lat_width, LANES), jnp.float32)
    for a in range(BACK):
        for r in range(rows):
            total = total + arrived[a, r]
    result_ref[...] = total

    for a in range(BACK):
        pl.when(t + a < frames)(lambda a=a: whole(window, a, lat_send, lat_recv).wait_send())
        pl.when(t >= a)(lambda a=a: whole(partial, a, part_send, part_recv).wait_send())


def on_device(frames, rows, latent, conv_weight, norm_gain, qkv_weight, out_weight, grad_out):
    lat_width = latent.shape[1]
    channels = grad_out.shape[3]
    taps = 27 * lat_width
    cells = rows * LANES
    chunk = min(cells, 512)
    bf16, f32 = jnp.bfloat16, jnp.float32
    flat = (
        latent.reshape(lat_width, LANES),
        conv_weight.reshape(taps, channels),
        norm_gain.reshape(1, channels),
        qkv_weight,
        out_weight,
        grad_out.reshape(LANES, channels),
    )
    scratch = [pltpu.VMEM(value.shape, value.dtype) for value in flat]
    scratch += [
        pltpu.VMEM((BACK, rows, lat_width, LANES), bf16),
        pltpu.VMEM((taps, cells), bf16),
        pltpu.VMEM((cells, channels), f32),
        pltpu.VMEM((cells, channels), bf16),
        pltpu.VMEM((channels, channels), bf16),
        pltpu.VMEM((2 * LANES, channels), bf16),
        pltpu.VMEM((cells, 2 * LANES), f32),
        pltpu.VMEM((cells, 2 * LANES), bf16),
        pltpu.VMEM((cells, channels), f32),
        pltpu.VMEM((cells, channels), bf16),
        pltpu.VMEM((taps, cells + 2 * LANES), f32),
        pltpu.VMEM((BACK, rows, lat_width, LANES), f32),
        pltpu.VMEM((BACK, rows, lat_width, LANES), f32),
        pltpu.SemaphoreType.DMA((6,)),
        pltpu.SemaphoreType.DMA((BACK,)),
        pltpu.SemaphoreType.DMA((BACK,)),
        pltpu.SemaphoreType.DMA((BACK,)),
        pltpu.SemaphoreType.DMA((BACK,)),
    ]
    result = pl.pallas_call(
        functools.partial(kernel, frames, rows, chunk),
        out_shape=jax.ShapeDtypeStruct((lat_width, LANES), f32),
        in_specs=[pl.BlockSpec(memory_space=pl.ANY)] * 6,
        out_specs=pl.BlockSpec(memory_space=pltpu.VMEM),
        scratch_shapes=scratch,
        compiler_params=pltpu.CompilerParams(
            collective_id=0, has_side_effects=True, vmem_limit_bytes=56 * 2**20
        ),
    )(*flat)
    return result.reshape(1, lat_width, 1, LANES)


def solution(mesh):
    return jax.shard_map(
        functools.partial(on_device, mesh.shape["tm"], mesh.shape["space"]),
        mesh=mesh,
        in_specs=(
            P(("group", "tm"), None, "space", None),
            P(),
            P(),
            P(),
            P(),
            P(("group", "tm"), "space", None, None),
        ),
        out_specs=P(("group", "tm"), None, "space", None),
        check_vma=False,
    )
```

```python
import functools

import jax
import jax.numpy as jnp
from jax import lax
from jax.experimental import pallas as pl
from jax.experimental.pallas import tpu as pltpu
from jax.sharding import PartitionSpec as P

GROUPS = 32
EPSILON = 1e-06
BACK = 3
LANES = 128
MESH = pl.DeviceIdType.MESH


def dot(left, right, left_dim, right_dim):
    return lax.dot_general(
        left, right, (((left_dim,), (right_dim,)), ((), ())), preferred_element_type=jnp.float32
    )


def group_sums(rows, per_group):
    channels = rows[0].shape[1]
    tiles = channels // LANES
    packed = jnp.concatenate(
        [row[:, k * LANES : (k + 1) * LANES] for row in rows for k in range(tiles)], axis=0
    )
    lane = lax.broadcasted_iota(jnp.int32, packed.shape, 1)
    step = 1
    while step < per_group:
        upper = pltpu.roll(packed, step, 1)
        lower = pltpu.roll(packed, LANES - step, 1)
        packed = packed + jnp.where((lane & step) != 0, upper, lower)
        step *= 2
    return [
        jnp.concatenate([packed[i * tiles + k : i * tiles + k + 1] for k in range(tiles)], axis=1)
        for i in range(len(rows))
    ]


def shifted(value, by):
    if by == 0:
        return value
    lane = lax.broadcasted_iota(jnp.int32, value.shape, 1)
    keep = lane < LANES - 1 if by == 1 else lane > 0
    return jnp.where(keep, pltpu.roll(value, (-by) % LANES, 1), 0.0)


def chunked(count, body, carry):
    if count == 1:
        return body(0, carry)
    return lax.fori_loop(0, count, body, carry)


def kernel(
    frames, rows, chunk,
    lat_hbm, conv_hbm, gain_hbm, qkv_hbm, out_hbm, grad_hbm,
    result_ref,
    lat, conv, gain, qkv, outw, grad,
    window, patches, hidden, normed, mixed, pair, scored, weights, grad_norm,
    grad_hid, columns, partial, arrived,
    load_sem, lat_send, lat_recv, part_send, part_recv,
):
    t = lax.axis_index("tm")
    me = lax.axis_index("space")
    lat_width = lat.shape[0]
    channels = grad.shape[1]
    per_group = channels // GROUPS
    cells = rows * LANES
    chunks = cells // chunk
    scaling = channels ** (-0.5)
    own = pl.ds(pl.multiple_of(me * LANES, LANES), LANES)

    loads = [
        pltpu.make_async_copy(source, target, load_sem.at[i])
        for i, (source, target) in enumerate(
            [(lat_hbm, lat), (grad_hbm, grad), (out_hbm, outw), (qkv_hbm, qkv), (conv_hbm, conv), (gain_hbm, gain)]
        )
    ]
    loads[0].start()

    def other(k):
        if k == rows - 1:
            return me
        upper = rows - 1 - k
        return jnp.where(2 * me >= rows, jnp.where(k >= me, k + 1, k), jnp.where(upper <= me, upper - 1, upper))

    barrier = pltpu.get_barrier_semaphore()
    def greet(step):
        for k in range(rows if step else rows - 1):
            pl.semaphore_signal(
                barrier, inc=1, device_id={"tm": t + step, "space": other(k)}, device_id_type=MESH
            )

    greet(0)
    for step in range(1, BACK):
        pl.when(t + step < frames)(functools.partial(greet, step))
        pl.when(t >= step)(functools.partial(greet, -step))
    for load in loads[1:]:
        load.start()

    loads[0].wait()
    window[0, me] = lat[...]
    for a in range(1, BACK):

        @pl.when(t < a)
        def _(a=a):
            window[a] = jnp.zeros(window.shape[1:], window.dtype)

    near = jnp.minimum(t, BACK - 1) + jnp.minimum(frames - 1 - t, BACK - 1) + 1
    pl.semaphore_wait(barrier, near * rows - 1)

    def send(source, target, send_sem, recv_sem, frame, row):
        return pltpu.make_async_remote_copy(
            src_ref=source, dst_ref=target, send_sem=send_sem, recv_sem=recv_sem,
            device_id={"tm": frame, "space": row}, device_id_type=MESH,
        )

    def whole(buffer, a, send_sem, recv_sem):
        block = buffer.at[a] if a else buffer.at[a, 0 : rows - 1]
        return send(block, block, send_sem.at[a], recv_sem.at[a], t, me)

    def send_latent(a, k):
        send(lat, window.at[a, me], lat_send.at[a], lat_recv.at[a], t + a, other(k)).start()

    for k in range(rows):
        for a in reversed(range(0 if k < rows - 1 else 1, BACK)):
            pl.when(t + a < frames)(functools.partial(send_latent, a, k))

    loads[1].wait()
    loads[2].wait()
    grad_att = dot(grad[...], outw[...], 1, 1).astype(jnp.bfloat16)
    loads[3].wait()
    pair[LANES:, :] = dot(grad_att, qkv[:, 2 * channels :], 1, 1).astype(jnp.bfloat16)
    mixed[...] = dot(qkv[:, :channels], qkv[:, channels : 2 * channels], 1, 1).astype(jnp.bfloat16)
    loads[4].wait()
    loads[5].wait()

    for a in range(BACK):
        pl.when(t >= a)(lambda a=a: whole(window, a, lat_send, lat_recv).wait_recv())

    zero_slab = jnp.zeros((3 * lat_width, LANES), jnp.bfloat16)
    for a in range(BACK):
        for r in range(rows):
            piece = window[a, r].astype(jnp.float32)
            for e in range(3):
                moved = shifted(piece, e - 1).astype(jnp.bfloat16)
                for b in range(3):
                    target = r - b + 1
                    if 0 <= target < rows:
                        tap = (a * 9 + b * 3 + e) * lat_width
                        patches[tap : tap + lat_width, target * LANES : (target + 1) * LANES] = moved
        first = a * 9 * lat_width
        patches[first : first + 3 * lat_width, 0:LANES] = zero_slab
        last = (a * 9 + 6) * lat_width
        patches[last : last + 3 * lat_width, (rows - 1) * LANES : rows * LANES] = zero_slab

    def rows_of(i):
        if isinstance(i, int):
            return pl.ds(i * chunk, chunk)
        return pl.ds(pl.multiple_of(i * chunk, chunk), chunk)

    zero_row = jnp.zeros((1, channels), jnp.float32)

    def convolve(i, total):
        part = dot(patches[:, rows_of(i)], conv[...], 0, 0)
        hidden[rows_of(i), :] = part
        return total + jnp.sum(part, axis=0, keepdims=True)

    count = float(cells * per_group)
    (average,) = group_sums([chunked(chunks, convolve, zero_row)], per_group)
    average = average / count

    def square(i, total):
        away = hidden[rows_of(i), :] - average
        return total + jnp.sum(away * away, axis=0, keepdims=True)

    (spread,) = group_sums([chunked(chunks, square, zero_row)], per_group)
    inverse = lax.rsqrt(spread / count + EPSILON)
    gains = gain[...]

    slope = inverse * gains

    def normalise(i, carry):
        normed[rows_of(i), :] = ((hidden[rows_of(i), :] - average) * slope).astype(jnp.bfloat16)
        return carry

    chunked(chunks, normalise, 0)

    pair[:LANES, :] = dot(normed[own, :], mixed[...], 1, 0).astype(jnp.bfloat16)

    def score(i, highest):
        part = dot(normed[rows_of(i), :], pair[...], 1, 1)
        scored[rows_of(i), :] = part
        return jnp.maximum(highest, jnp.max(part[:, :LANES], axis=0, keepdims=True))

    highest = chunked(chunks, score, jnp.full((1, LANES), -jnp.inf, jnp.float32))

    def exponent(i, total):
        part = jnp.exp((scored[rows_of(i), :LANES] - highest) * scaling)
        scored[rows_of(i), :LANES] = part
        return total + jnp.sum(part, axis=0, keepdims=True)

    share = 1.0 / chunked(chunks, exponent, jnp.zeros((1, LANES), jnp.float32))

    def normal(i, total):
        part = scored[rows_of(i), :LANES] * share
        scored[rows_of(i), :LANES] = part
        rounded = part.astype(jnp.bfloat16)
        weights[rows_of(i), LANES:] = rounded
        return total + jnp.sum(rounded.astype(jnp.float32) * scored[rows_of(i), LANES:], axis=0, keepdims=True)

    delta = chunked(chunks, normal, jnp.zeros((1, LANES), jnp.float32))

    def backward(i, total):
        part = scored[rows_of(i), :LANES] * (scored[rows_of(i), LANES:] - delta) * scaling
        rounded = part.astype(jnp.bfloat16)
        weights[rows_of(i), :LANES] = rounded
        grad_norm[rows_of(i), :] = dot(weights[rows_of(i), :], pair[...], 1, 0)
        return total + dot(rounded, normed[rows_of(i), :], 0, 0)

    pulled = chunked(chunks, backward, jnp.zeros((LANES, channels), jnp.float32))
    grad_norm[own, :] += dot(pulled.astype(jnp.bfloat16), mixed[...], 1, 1)

    def moments(i, carry):
        first, second = carry
        part = grad_norm[rows_of(i), :]
        first = first + jnp.sum(part, axis=0, keepdims=True)
        second = second + jnp.sum(part * (hidden[rows_of(i), :] - average), axis=0, keepdims=True)
        return first, second

    first, second = chunked(chunks, moments, (zero_row, zero_row))
    first, second = group_sums([first * gains, second * slope], per_group)
    first = first / count
    second = second / count

    tilt = second * inverse * inverse
    offset = average * tilt - first * inverse

    def hidden_grad(where):
        return grad_norm[where, :] * slope - hidden[where, :] * tilt + offset

    def finish(i, carry):
        grad_hid[rows_of(i), :] = hidden_grad(rows_of(i)).astype(jnp.bfloat16)
        return carry

    chunked(chunks, finish, 0)
    grad_hid[own, :] = (grad[...].astype(jnp.float32) + hidden_grad(own)).astype(jnp.bfloat16)

    columns[:, 0:LANES] = jnp.zeros((columns.shape[0], LANES), jnp.float32)
    columns[:, (rows + 1) * LANES :] = jnp.zeros((columns.shape[0], LANES), jnp.float32)

    def spread_taps(i, carry):
        if isinstance(i, int):
            where = pl.ds(LANES + i * chunk, chunk)
        else:
            where = pl.ds(pl.multiple_of(LANES + i * chunk, LANES), chunk)
        columns[:, where] = dot(conv[...], grad_hid[rows_of(i), :], 1, 1)
        return carry

    chunked(chunks, spread_taps, 0)

    def send_partial(a):
        for k in range(rows if a else rows - 1):
            row = other(k)
            send(partial.at[a, row], arrived.at[a, me], part_send.at[a], part_recv.at[a], t - a, row).start()

    for a in reversed(range(BACK)):
        for y in range(rows):
            total = jnp.zeros((lat_width, LANES), jnp.float32)
            for e in range(3):
                inner = jnp.zeros((lat_width, LANES), jnp.float32)
                for b in range(3):
                    tap = (a * 9 + b * 3 + e) * lat_width
                    at = (y - b + 2) * LANES
                    inner = inner + columns[tap : tap + lat_width, at : at + LANES]
                total = total + shifted(inner, 1 - e)
            partial[a, y] = total
        pl.when(t >= a)(functools.partial(send_partial, a))

    arrived[0, me] = partial[0, me]
    for a in range(1, BACK):

        @pl.when(t + a >= frames)
        def _(a=a):
            arrived[a] = jnp.zeros(arrived.shape[1:], arrived.dtype)

    for a in range(BACK):
        pl.when(t + a < frames)(lambda a=a: whole(arrived, a, part_send, part_recv).wait_recv())

    total = jnp.zeros((lat_width, LANES), jnp.float32)
    for a in range(BACK):
        for r in range(rows):
            total = total + arrived[a, r]
    result_ref[...] = total

    for a in range(BACK):
        pl.when(t + a < frames)(lambda a=a: whole(window, a, lat_send, lat_recv).wait_send())
        pl.when(t >= a)(lambda a=a: whole(partial, a, part_send, part_recv).wait_send())


def on_device(frames, rows, latent, conv_weight, norm_gain, qkv_weight, out_weight, grad_out):
    lat_width = latent.shape[1]
    channels = grad_out.shape[3]
    taps = 27 * lat_width
    cells = rows * LANES
    chunk = min(cells, 512)
    bf16, f32 = jnp.bfloat16, jnp.float32
    flat = (
        latent.reshape(lat_width, LANES),
        conv_weight.reshape(taps, channels),
        norm_gain.reshape(1, channels),
        qkv_weight,
        out_weight,
        grad_out.reshape(LANES, channels),
    )
    scratch = [pltpu.VMEM(value.shape, value.dtype) for value in flat]
    scratch += [
        pltpu.VMEM((BACK, rows, lat_width, LANES), bf16),
        pltpu.VMEM((taps, cells), bf16),
        pltpu.VMEM((cells, channels), f32),
        pltpu.VMEM((cells, channels), bf16),
        pltpu.VMEM((channels, channels), bf16),
        pltpu.VMEM((2 * LANES, channels), bf16),
        pltpu.VMEM((cells, 2 * LANES), f32),
        pltpu.VMEM((cells, 2 * LANES), bf16),
        pltpu.VMEM((cells, channels), f32),
        pltpu.VMEM((cells, channels), bf16),
        pltpu.VMEM((taps, cells + 2 * LANES), f32),
        pltpu.VMEM((BACK, rows, lat_width, LANES), f32),
        pltpu.VMEM((BACK, rows, lat_width, LANES), f32),
        pltpu.SemaphoreType.DMA((6,)),
        pltpu.SemaphoreType.DMA((BACK,)),
        pltpu.SemaphoreType.DMA((BACK,)),
        pltpu.SemaphoreType.DMA((BACK,)),
        pltpu.SemaphoreType.DMA((BACK,)),
    ]
    result = pl.pallas_call(
        functools.partial(kernel, frames, rows, chunk),
        out_shape=pltpu.VMEM((lat_width, LANES), f32),
        in_specs=[pl.BlockSpec(memory_space=pl.ANY)] * 6,
        out_specs=pl.BlockSpec(memory_space=pltpu.VMEM),
        scratch_shapes=scratch,
        compiler_params=pltpu.CompilerParams(
            collective_id=0, has_side_effects=True, vmem_limit_bytes=56 * 2**20
        ),
    )(*flat)
    return result.reshape(1, lat_width, 1, LANES)


def solution(mesh):
    return jax.shard_map(
        functools.partial(on_device, mesh.shape["tm"], mesh.shape["space"]),
        mesh=mesh,
        in_specs=(
            P(("group", "tm"), None, "space", None),
            P(),
            P(),
            P(),
            P(),
            P(("group", "tm"), "space", None, None),
        ),
        out_specs=P(("group", "tm"), None, "space", None),
        check_vma=False,
    )
```

```python
import functools

import jax
import jax.numpy as jnp
from jax import lax
from jax.experimental import pallas as pl
from jax.experimental.pallas import tpu as pltpu
from jax.sharding import PartitionSpec as P

GROUPS = 32
EPSILON = 1e-06
BACK = 3
LANES = 128
MESH = pl.DeviceIdType.MESH


def dot(left, right, left_dim, right_dim):
    return lax.dot_general(
        left, right, (((left_dim,), (right_dim,)), ((), ())), preferred_element_type=jnp.float32
    )


def group_sums(rows, per_group):
    channels = rows[0].shape[1]
    tiles = channels // LANES
    packed = jnp.concatenate(
        [row[:, k * LANES : (k + 1) * LANES] for row in rows for k in range(tiles)], axis=0
    )
    lane = lax.broadcasted_iota(jnp.int32, packed.shape, 1)
    step = 1
    while step < per_group:
        upper = pltpu.roll(packed, step, 1)
        lower = pltpu.roll(packed, LANES - step, 1)
        packed = packed + jnp.where((lane & step) != 0, upper, lower)
        step *= 2
    return [
        jnp.concatenate([packed[i * tiles + k : i * tiles + k + 1] for k in range(tiles)], axis=1)
        for i in range(len(rows))
    ]


def shifted(value, by):
    if by == 0:
        return value
    lane = lax.broadcasted_iota(jnp.int32, value.shape, 1)
    keep = lane < LANES - 1 if by == 1 else lane > 0
    return jnp.where(keep, pltpu.roll(value, (-by) % LANES, 1), 0.0)


def chunked(count, body, carry):
    if count <= 4:
        for i in range(count):
            carry = body(i, carry)
        return carry
    return lax.fori_loop(0, count, body, carry)


def kernel(
    frames, rows, chunk,
    lat_hbm, conv_hbm, gain_hbm, qkv_hbm, out_hbm, grad_hbm,
    result_ref,
    lat, conv, gain, qkv, outw, grad,
    window, patches, hidden, normed, mixed, pair, scored, weights, grad_norm,
    grad_hid, columns, partial, arrived,
    load_sem, lat_send, lat_recv, part_send, part_recv,
):
    t = lax.axis_index("tm")
    me = lax.axis_index("space")
    lat_width = lat.shape[0]
    channels = grad.shape[1]
    per_group = channels // GROUPS
    cells = rows * LANES
    chunks = cells // chunk
    scaling = channels ** (-0.5)
    own = pl.ds(pl.multiple_of(me * LANES, LANES), LANES)

    loads = [
        pltpu.make_async_copy(source, target, load_sem.at[i])
        for i, (source, target) in enumerate(
            [(lat_hbm, lat), (grad_hbm, grad), (out_hbm, outw), (qkv_hbm, qkv), (conv_hbm, conv), (gain_hbm, gain)]
        )
    ]
    loads[0].start()

    def other(k):
        if k == rows - 1:
            return me
        upper = rows - 1 - k
        return jnp.where(2 * me >= rows, jnp.where(k >= me, k + 1, k), jnp.where(upper <= me, upper - 1, upper))

    barrier = pltpu.get_barrier_semaphore()
    def greet(step):
        for k in range(rows if step else rows - 1):
            pl.semaphore_signal(
                barrier, inc=1, device_id={"tm": t + step, "space": other(k)}, device_id_type=MESH
            )

    greet(0)
    for step in range(1, BACK):
        pl.when(t + step < frames)(functools.partial(greet, step))
        pl.when(t >= step)(functools.partial(greet, -step))
    for load in loads[1:]:
        load.start()

    loads[0].wait()
    window[0, me] = lat[...]
    for a in range(1, BACK):

        @pl.when(t < a)
        def _(a=a):
            window[a] = jnp.zeros(window.shape[1:], window.dtype)

    near = jnp.minimum(t, BACK - 1) + jnp.minimum(frames - 1 - t, BACK - 1) + 1
    pl.semaphore_wait(barrier, near * rows - 1)

    def send(source, target, send_sem, recv_sem, frame, row):
        return pltpu.make_async_remote_copy(
            src_ref=source, dst_ref=target, send_sem=send_sem, recv_sem=recv_sem,
            device_id={"tm": frame, "space": row}, device_id_type=MESH,
        )

    def whole(buffer, a, send_sem, recv_sem):
        block = buffer.at[a] if a else buffer.at[a, 0 : rows - 1]
        return send(block, block, send_sem.at[a], recv_sem.at[a], t, me)

    def send_latent(a, k):
        send(lat, window.at[a, me], lat_send.at[a], lat_recv.at[a], t + a, other(k)).start()

    for k in range(rows):
        for a in reversed(range(0 if k < rows - 1 else 1, BACK)):
            pl.when(t + a < frames)(functools.partial(send_latent, a, k))

    loads[1].wait()
    loads[2].wait()
    grad_att = dot(grad[...], outw[...], 1, 1).astype(jnp.bfloat16)
    loads[3].wait()
    pair[LANES:, :] = dot(grad_att, qkv[:, 2 * channels :], 1, 1).astype(jnp.bfloat16)
    mixed[...] = dot(qkv[:, :channels], qkv[:, channels : 2 * channels], 1, 1).astype(jnp.bfloat16)
    loads[4].wait()
    loads[5].wait()

    for a in range(BACK):
        pl.when(t >= a)(lambda a=a: whole(window, a, lat_send, lat_recv).wait_recv())

    zero_slab = jnp.zeros((3 * lat_width, LANES), jnp.bfloat16)
    for a in range(BACK):
        for r in range(rows):
            piece = window[a, r].astype(jnp.float32)
            for e in range(3):
                moved = shifted(piece, e - 1).astype(jnp.bfloat16)
                for b in range(3):
                    target = r - b + 1
                    if 0 <= target < rows:
                        tap = (a * 9 + b * 3 + e) * lat_width
                        patches[tap : tap + lat_width, target * LANES : (target + 1) * LANES] = moved
        first = a * 9 * lat_width
        patches[first : first + 3 * lat_width, 0:LANES] = zero_slab
        last = (a * 9 + 6) * lat_width
        patches[last : last + 3 * lat_width, (rows - 1) * LANES : rows * LANES] = zero_slab

    def rows_of(i):
        if isinstance(i, int):
            return pl.ds(i * chunk, chunk)
        return pl.ds(pl.multiple_of(i * chunk, chunk), chunk)

    zero_row = jnp.zeros((1, channels), jnp.float32)

    def convolve(i, total):
        part = dot(patches[:, rows_of(i)], conv[...], 0, 0)
        hidden[rows_of(i), :] = part
        return total + jnp.sum(part, axis=0, keepdims=True)

    count = float(cells * per_group)
    (average,) = group_sums([chunked(chunks, convolve, zero_row)], per_group)
    average = average / count

    def square(i, total):
        away = hidden[rows_of(i), :] - average
        return total + jnp.sum(away * away, axis=0, keepdims=True)

    (spread,) = group_sums([chunked(chunks, square, zero_row)], per_group)
    inverse = lax.rsqrt(spread / count + EPSILON)
    gains = gain[...]

    slope = inverse * gains

    def normalise(i, carry):
        normed[rows_of(i), :] = ((hidden[rows_of(i), :] - average) * slope).astype(jnp.bfloat16)
        return carry

    chunked(chunks, normalise, 0)

    pair[:LANES, :] = dot(normed[own, :], mixed[...], 1, 0).astype(jnp.bfloat16)

    def score(i, highest):
        part = dot(normed[rows_of(i), :], pair[...], 1, 1)
        scored[rows_of(i), :] = part
        return jnp.maximum(highest, jnp.max(part[:, :LANES], axis=0, keepdims=True))

    highest = chunked(chunks, score, jnp.full((1, LANES), -jnp.inf, jnp.float32))

    def exponent(i, total):
        part = jnp.exp((scored[rows_of(i), :LANES] - highest) * scaling)
        scored[rows_of(i), :LANES] = part
        return total + jnp.sum(part, axis=0, keepdims=True)

    share = 1.0 / chunked(chunks, exponent, jnp.zeros((1, LANES), jnp.float32))

    def normal(i, total):
        part = scored[rows_of(i), :LANES] * share
        scored[rows_of(i), :LANES] = part
        rounded = part.astype(jnp.bfloat16)
        weights[rows_of(i), LANES:] = rounded
        return total + jnp.sum(rounded.astype(jnp.float32) * scored[rows_of(i), LANES:], axis=0, keepdims=True)

    delta = chunked(chunks, normal, jnp.zeros((1, LANES), jnp.float32))

    def backward(i, total):
        part = scored[rows_of(i), :LANES] * (scored[rows_of(i), LANES:] - delta) * scaling
        rounded = part.astype(jnp.bfloat16)
        weights[rows_of(i), :LANES] = rounded
        grad_norm[rows_of(i), :] = dot(weights[rows_of(i), :], pair[...], 1, 0)
        return total + dot(rounded, normed[rows_of(i), :], 0, 0)

    pulled = chunked(chunks, backward, jnp.zeros((LANES, channels), jnp.float32))
    grad_norm[own, :] += dot(pulled.astype(jnp.bfloat16), mixed[...], 1, 1)

    def moments(i, carry):
        first, second = carry
        part = grad_norm[rows_of(i), :]
        first = first + jnp.sum(part, axis=0, keepdims=True)
        second = second + jnp.sum(part * (hidden[rows_of(i), :] - average), axis=0, keepdims=True)
        return first, second

    first, second = chunked(chunks, moments, (zero_row, zero_row))
    first, second = group_sums([first * gains, second * slope], per_group)
    first = first / count
    second = second / count

    tilt = second * inverse * inverse
    offset = average * tilt - first * inverse

    def hidden_grad(where):
        return grad_norm[where, :] * slope - hidden[where, :] * tilt + offset

    def finish(i, carry):
        grad_hid[rows_of(i), :] = hidden_grad(rows_of(i)).astype(jnp.bfloat16)
        return carry

    chunked(chunks, finish, 0)
    grad_hid[own, :] = (grad[...].astype(jnp.float32) + hidden_grad(own)).astype(jnp.bfloat16)

    columns[:, 0:LANES] = jnp.zeros((columns.shape[0], LANES), jnp.float32)
    columns[:, (rows + 1) * LANES :] = jnp.zeros((columns.shape[0], LANES), jnp.float32)

    def spread_taps(i, carry):
        if isinstance(i, int):
            where = pl.ds(LANES + i * chunk, chunk)
        else:
            where = pl.ds(pl.multiple_of(LANES + i * chunk, LANES), chunk)
        columns[:, where] = dot(conv[...], grad_hid[rows_of(i), :], 1, 1)
        return carry

    chunked(chunks, spread_taps, 0)

    def send_partial(a):
        for k in range(rows if a else rows - 1):
            row = other(k)
            send(partial.at[a, row], arrived.at[a, me], part_send.at[a], part_recv.at[a], t - a, row).start()

    for a in reversed(range(BACK)):
        for y in range(rows):
            total = jnp.zeros((lat_width, LANES), jnp.float32)
            for e in range(3):
                inner = jnp.zeros((lat_width, LANES), jnp.float32)
                for b in range(3):
                    tap = (a * 9 + b * 3 + e) * lat_width
                    at = (y - b + 2) * LANES
                    inner = inner + columns[tap : tap + lat_width, at : at + LANES]
                total = total + shifted(inner, 1 - e)
            partial[a, y] = total
        pl.when(t >= a)(functools.partial(send_partial, a))

    arrived[0, me] = partial[0, me]
    for a in range(1, BACK):

        @pl.when(t + a >= frames)
        def _(a=a):
            arrived[a] = jnp.zeros(arrived.shape[1:], arrived.dtype)

    for a in range(BACK):
        pl.when(t + a < frames)(lambda a=a: whole(arrived, a, part_send, part_recv).wait_recv())

    total = jnp.zeros((lat_width, LANES), jnp.float32)
    for a in range(BACK):
        for r in range(rows):
            total = total + arrived[a, r]
    result_ref[...] = total

    for a in range(BACK):
        pl.when(t + a < frames)(lambda a=a: whole(window, a, lat_send, lat_recv).wait_send())
        pl.when(t >= a)(lambda a=a: whole(partial, a, part_send, part_recv).wait_send())


def on_device(frames, rows, latent, conv_weight, norm_gain, qkv_weight, out_weight, grad_out):
    lat_width = latent.shape[1]
    channels = grad_out.shape[3]
    taps = 27 * lat_width
    cells = rows * LANES
    chunk = min(cells, 256)
    bf16, f32 = jnp.bfloat16, jnp.float32
    flat = (
        latent.reshape(lat_width, LANES),
        conv_weight.reshape(taps, channels),
        norm_gain.reshape(1, channels),
        qkv_weight,
        out_weight,
        grad_out.reshape(LANES, channels),
    )
    scratch = [pltpu.VMEM(value.shape, value.dtype) for value in flat]
    scratch += [
        pltpu.VMEM((BACK, rows, lat_width, LANES), bf16),
        pltpu.VMEM((taps, cells), bf16),
        pltpu.VMEM((cells, channels), f32),
        pltpu.VMEM((cells, channels), bf16),
        pltpu.VMEM((channels, channels), bf16),
        pltpu.VMEM((2 * LANES, channels), bf16),
        pltpu.VMEM((cells, 2 * LANES), f32),
        pltpu.VMEM((cells, 2 * LANES), bf16),
        pltpu.VMEM((cells, channels), f32),
        pltpu.VMEM((cells, channels), bf16),
        pltpu.VMEM((taps, cells + 2 * LANES), f32),
        pltpu.VMEM((BACK, rows, lat_width, LANES), f32),
        pltpu.VMEM((BACK, rows, lat_width, LANES), f32),
        pltpu.SemaphoreType.DMA((6,)),
        pltpu.SemaphoreType.DMA((BACK,)),
        pltpu.SemaphoreType.DMA((BACK,)),
        pltpu.SemaphoreType.DMA((BACK,)),
        pltpu.SemaphoreType.DMA((BACK,)),
    ]
    result = pl.pallas_call(
        functools.partial(kernel, frames, rows, chunk),
        out_shape=pltpu.VMEM((lat_width, LANES), f32),
        in_specs=[pl.BlockSpec(memory_space=pl.ANY)] * 6,
        out_specs=pl.BlockSpec(memory_space=pltpu.VMEM),
        scratch_shapes=scratch,
        compiler_params=pltpu.CompilerParams(
            collective_id=0, has_side_effects=True, vmem_limit_bytes=56 * 2**20
        ),
    )(*flat)
    return result.reshape(1, lat_width, 1, LANES)


def solution(mesh):
    return jax.shard_map(
        functools.partial(on_device, mesh.shape["tm"], mesh.shape["space"]),
        mesh=mesh,
        in_specs=(
            P(("group", "tm"), None, "space", None),
            P(),
            P(),
            P(),
            P(),
            P(("group", "tm"), "space", None, None),
        ),
        out_specs=P(("group", "tm"), None, "space", None),
        check_vma=False,
    )
```
